128 devices in a mesh: seq: 16 (over z, x), req: 8 (over y, core).
Axes of the slice: x: 4, y: 4, z: 4, core: 2. Of those that a mesh axis runs over, the one named last changes fastest.
Arguments:
- q_new: bfloat16 [128, 4, 2048], P('req')
- fresh_keys: bfloat16 [128, 4, 1024], P('req')
- fresh_values: bfloat16 [128, 4, 1024], P('req'), may hold values from -6 to 6
- q_gain: float32 [256], replicated, may hold values from 0.1 to 1.9
- prompt_key_cache: bfloat16 [16, 15360, 1024], P('req', 'seq')
- prompt_value_cache: bfloat16 [16, 15360, 1024], P('req', 'seq'), may hold values from -6 to 6
- tail_key_cache: bfloat16 [128, 1024, 1024], P('req', 'seq')
- tail_value_cache: bfloat16 [128, 1024, 1024], P('req', 'seq'), may hold values from -6 to 6
- group_of: int32 [128], P('req'), may hold values from 0 to 1, as said below
- prefix_len: int32 [16], P('req'), may hold values from 1 to 15360, as said below
- tail_len: int32 [128], P('req'), may hold values from 1 to 1024, as said below
- resid: bfloat16 [128, 4, 2560], P('req'), may hold values from -6 to 6
- w_out: bfloat16 [2048, 2560], replicated, may hold values from -0.125 to 0.125
- attn_gain: float32 [2560], replicated, may hold values from 0.1 to 1.9
- pre_gain: float32 [2560], replicated, may hold values from 0.1 to 1.9
- post_gain: float32 [2560], replicated, may hold values from 0.1 to 1.9
- w_gate: bfloat16 [2560, 10240], P(None, ('seq', 'req')), may hold values from -0.125 to 0.125
- w_up: bfloat16 [2560, 10240], P(None, ('seq', 'req')), may hold values from -0.125 to 0.125
- w_down: bfloat16 [10240, 2560], P(('seq', 'req')), may hold values from -0.0625 to 0.0625
Outputs:
- out: bfloat16 [128, 4, 2560], P(('req', 'seq'))
The draws below stay inside these ranges and needn't reach their ends.
Inputs may be any that keep to these rules, and one draw needn't show every extreme that they name: `group_of`: requests 16 * b to 16 * b + 15 form one block whose groups are 2 * b onward; each of the two groups of a block has at least 4 requests. `prefix_len`: in every block of 2 groups one prompt fills its cache. `tail_len`: in every block of 16 requests one tail fills its cache.
All inputs are finite; a program needn't handle non-finite values.
Results may differ from the reference program's by a relative error of at most 0.015.
The reference program's roundings to bfloat16 on the way count: a program that leaves them out, or rounds other values in their place, can miss the bound.
Values may be sent and summed in bfloat16 or wider, within the bound.
A program may use at most 128 MiB of HBM per device.

```python
import math
import jax
import jax.numpy as jnp
from jax import lax

D = 2560
FF = 10240
QUERY_HEADS = 8
KEY_VALUE_HEADS = 4
HEAD_SIZE = 256
DECODE_STEPS = 4
R_DEV = 16
GROUPS_DEV = 2
REQUEST_COUNT = 128
PROMPT_GROUPS = 16
PROMPT_CAPACITY = 15360
TAIL_CAPACITY = 1024
TOKENS = 512


def joint_new(key):
    rotary_base = jax.random.fold_in(key, 7)
    first_half, second_half = jax.random.split(rotary_base)
    query_rows = jax.random.normal(first_half, (REQUEST_COUNT, DECODE_STEPS, QUERY_HEADS * HEAD_SIZE), jnp.float32)
    noise_draw = jax.random.normal(second_half, (REQUEST_COUNT, DECODE_STEPS, KEY_VALUE_HEADS, HEAD_SIZE), jnp.float32)
    leading_shape = query_rows.reshape(REQUEST_COUNT, DECODE_STEPS, KEY_VALUE_HEADS, QUERY_HEADS // KEY_VALUE_HEADS, HEAD_SIZE)[:, :, :, 0, :]
    key_rows = 0.6 * leading_shape + 0.8 * noise_draw
    return (query_rows, key_rows.reshape(REQUEST_COUNT, DECODE_STEPS, KEY_VALUE_HEADS * HEAD_SIZE))


def draw_q_new(key, part):
    return joint_new(key)[0].astype(jnp.bfloat16)


def draw_fresh_keys(key, part):
    return joint_new(key)[1].astype(jnp.bfloat16)


def scaled_keys(key, leading_shape, length_value, salt):
    first_half, second_half = jax.random.split(jax.random.fold_in(key, salt))
    rotary_base = jax.random.normal(first_half, (leading_shape, length_value, KEY_VALUE_HEADS, HEAD_SIZE), jnp.float32)
    spread_heads = jax.random.uniform(second_half, (leading_shape, length_value, KEY_VALUE_HEADS, 1), jnp.float32, math.log(0.3), math.log(3.0))
    return (rotary_base * jnp.exp(spread_heads)).reshape(leading_shape, length_value, KEY_VALUE_HEADS * HEAD_SIZE)


def draw_prompt_key_cache(key, part):
    return scaled_keys(key, PROMPT_GROUPS, PROMPT_CAPACITY, 11).astype(jnp.bfloat16)


def draw_tail_key_cache(key, part):
    return scaled_keys(key, REQUEST_COUNT, TAIL_CAPACITY, 13).astype(jnp.bfloat16)


def draw_group_of(key, part):
    block_keys = jax.random.split(jax.random.fold_in(key, 3), REQUEST_COUNT // R_DEV)

    def one_block(block_key):
        first_half, second_half = jax.random.split(block_key)
        order = jax.random.permutation(first_half, R_DEV)
        split_point = jax.random.randint(second_half, (), 4, R_DEV - 3)
        return (order >= split_point).astype(jnp.int32)
    return jax.vmap(one_block)(block_keys).reshape(REQUEST_COUNT)


def filled_lengths(key, salt, blocks, width, most):
    first_half, second_half = jax.random.split(jax.random.fold_in(key, salt))
    lengths = jax.random.randint(first_half, (blocks, width), 1, most + 1)
    chosen = jax.random.randint(second_half, (blocks, 1), 0, width)
    lengths = jnp.where(jnp.arange(width, dtype=jnp.int32)[None, :] == chosen, most, lengths)
    return lengths.reshape(blocks * width).astype(jnp.int32)


def draw_prefix_len(key, part):
    return filled_lengths(key, 5, REQUEST_COUNT // R_DEV, GROUPS_DEV, PROMPT_CAPACITY)


def draw_tail_len(key, part):
    return filled_lengths(key, 9, REQUEST_COUNT // R_DEV, R_DEV, TAIL_CAPACITY)


def levels(rng, dims, shards, low, high):
    level, own = 1.0, jax.random.fold_in(rng, 6)
    for dim, shards_of in shards:
        heights = jnp.exp(jax.random.uniform(jax.random.fold_in(own, dim), (shards_of,), jnp.float32, low / len(shards), high / len(shards)))
        level = level * jnp.repeat(heights, dims[dim] // shards_of).reshape([-1 if axis == dim else 1 for axis in range(len(dims))])
    return level


def centred(stream_key, dims, deviation, reach, shards=(), kind=jnp.bfloat16):
    loudness = levels(stream_key, dims, shards, -0.22, 0.18) if shards else 1.0
    entries = jax.random.normal(stream_key, dims, jnp.float32) * deviation * loudness
    return jnp.minimum(jnp.maximum(entries, -reach), reach).astype(kind)


def setup_inputs(seed: int = 0) -> dict:
    splits = jax.random.split(jax.random.key(seed), 20)
    return {
        "q_new": draw_q_new(jax.random.fold_in(splits[19], 71), 0),
        "fresh_keys": draw_fresh_keys(jax.random.fold_in(splits[19], 71), 0),
        "fresh_values": centred(splits[2], (REQUEST_COUNT, DECODE_STEPS, KEY_VALUE_HEADS * HEAD_SIZE), 1.0, 6.0, ((0, 8),)),
        "q_gain": jnp.clip(1.0 + 0.18 * jax.random.normal(splits[3], (HEAD_SIZE,), jnp.float32), 0.1, 1.9),
        "prompt_key_cache": draw_prompt_key_cache(jax.random.fold_in(splits[19], 71), 0),
        "prompt_value_cache": centred(splits[5], (PROMPT_GROUPS, PROMPT_CAPACITY, KEY_VALUE_HEADS * HEAD_SIZE), 1.0, 6.0, ((0, 8), (1, 16))),
        "tail_key_cache": draw_tail_key_cache(jax.random.fold_in(splits[19], 71), 0),
        "tail_value_cache": centred(splits[7], (REQUEST_COUNT, TAIL_CAPACITY, KEY_VALUE_HEADS * HEAD_SIZE), 1.0, 6.0, ((0, 8), (1, 16))),
        "group_of": draw_group_of(jax.random.fold_in(splits[19], 71), 0),
        "prefix_len": draw_prefix_len(jax.random.fold_in(splits[19], 71), 0),
        "tail_len": draw_tail_len(jax.random.fold_in(splits[19], 71), 0),
        "resid": centred(splits[11], (REQUEST_COUNT, DECODE_STEPS, D), 1.0, 6.0, ((0, 8),)),
        "w_out": centred(splits[12], (QUERY_HEADS * HEAD_SIZE, D), (QUERY_HEADS * HEAD_SIZE) ** -0.5, 0.125),
        "attn_gain": jnp.clip(1.0 + 0.18 * jax.random.normal(splits[13], (D,), jnp.float32), 0.1, 1.9),
        "pre_gain": jnp.clip(1.0 + 0.18 * jax.random.normal(splits[14], (D,), jnp.float32), 0.1, 1.9),
        "post_gain": jnp.clip(1.0 + 0.18 * jax.random.normal(splits[15], (D,), jnp.float32), 0.1, 1.9),
        "w_gate": centred(splits[16], (D, FF), D ** -0.5, 0.125, ((1, 128),)),
        "w_up": centred(splits[17], (D, FF), D ** -0.5, 0.125, ((1, 128),)),
        "w_down": centred(splits[18], (FF, D), FF ** -0.5, 0.0625, ((0, 128),)),
    }


eps = 1e-06
theta = 1000000.0

def scale_for_norm(value_rows, gain):
    mean_square = lax.optimization_barrier(jnp.mean(value_rows * value_rows, axis=-1, keepdims=True))
    return value_rows * lax.rsqrt(mean_square + eps) * gain

def apply_rotary(value_rows, token_positions):
    half = value_rows.shape[-1] // 2
    freq = theta ** (-(jnp.arange(half, dtype=jnp.float32) * 2.0 / value_rows.shape[-1]))
    angle = token_positions[..., None] * freq
    cosine = jnp.cos(angle)
    sine = jnp.sin(angle)
    first_half = value_rows[..., :half]
    second_half = value_rows[..., half:]
    return jnp.concatenate([first_half * cosine - second_half * sine, second_half * cosine + first_half * sine], axis=-1)

def reference(q_new, fresh_keys, fresh_values, q_gain, prompt_key_cache, prompt_value_cache, tail_key_cache, tail_value_cache, group_of, prefix_len, tail_len, resid, w_out, attn_gain, pre_gain, post_gain, w_gate, w_up, w_down):
    head_repeats = QUERY_HEADS // KEY_VALUE_HEADS
    step_index = jnp.arange(DECODE_STEPS, dtype=jnp.int32)

    def one_request(index_value):
        group_index = (index_value // R_DEV * GROUPS_DEV + group_of[index_value]).astype(jnp.int32)
        prompt_end = prefix_len[group_index]
        tail_end = tail_len[index_value]
        token_positions = (prompt_end + tail_end + step_index).astype(jnp.float32)
        query_rows = scale_for_norm(q_new[index_value].astype(jnp.float32).reshape(DECODE_STEPS, QUERY_HEADS, HEAD_SIZE), q_gain)
        query_rows = apply_rotary(query_rows, token_positions[:, None]) * HEAD_SIZE ** (-0.5)
        query_rows = query_rows.astype(jnp.bfloat16).reshape(DECODE_STEPS, KEY_VALUE_HEADS, head_repeats, HEAD_SIZE)
        request_key = apply_rotary(scale_for_norm(fresh_keys[index_value].astype(jnp.float32).reshape(DECODE_STEPS, KEY_VALUE_HEADS, HEAD_SIZE), 1.0), token_positions[:, None]).astype(jnp.bfloat16)
        key_rows = jnp.concatenate([prompt_key_cache[group_index].reshape(PROMPT_CAPACITY, KEY_VALUE_HEADS, HEAD_SIZE), tail_key_cache[index_value].reshape(TAIL_CAPACITY, KEY_VALUE_HEADS, HEAD_SIZE), request_key], axis=0)
        value_rows = jnp.concatenate([prompt_value_cache[group_index].reshape(PROMPT_CAPACITY, KEY_VALUE_HEADS, HEAD_SIZE), tail_value_cache[index_value].reshape(TAIL_CAPACITY, KEY_VALUE_HEADS, HEAD_SIZE), fresh_values[index_value].reshape(DECODE_STEPS, KEY_VALUE_HEADS, HEAD_SIZE)], axis=0)
        scores = jnp.einsum('skqd,jkd->skqj', query_rows.astype(jnp.float32), key_rows.astype(jnp.float32))
        slot = jnp.arange(PROMPT_CAPACITY + TAIL_CAPACITY + DECODE_STEPS, dtype=jnp.int32)
        cached = (slot < prompt_end) | (slot >= PROMPT_CAPACITY) & (slot - PROMPT_CAPACITY < tail_end) & (slot < PROMPT_CAPACITY + TAIL_CAPACITY)
        own = slot - PROMPT_CAPACITY - TAIL_CAPACITY
        own_ok = (own[None, :] >= 0) & (own[None, :] <= step_index[:, None])
        valid = (cached[None, :] | own_ok)[:, None, None, :]
        masked = jnp.where(valid, scores, -jnp.inf)
        peak = lax.optimization_barrier(jnp.max(masked, axis=-1, keepdims=True))
        prob = jnp.where(valid, jnp.exp(scores - peak), 0.0)
        total = lax.optimization_barrier(jnp.sum(prob, axis=-1))
        weights = prob.astype(jnp.bfloat16)
        mixed = jnp.einsum('skqj,jkd->skqd', weights.astype(jnp.float32), value_rows.astype(jnp.float32)) / total[..., None]
        return mixed.reshape(DECODE_STEPS, QUERY_HEADS * HEAD_SIZE)
    mixed_all = lax.map(one_request, jnp.arange(REQUEST_COUNT, dtype=jnp.int32))
    heads = mixed_all.astype(jnp.bfloat16).reshape(TOKENS, QUERY_HEADS * HEAD_SIZE)
    proj = jnp.dot(heads, w_out, preferred_element_type=jnp.float32)
    hstate = (resid.reshape(TOKENS, D).astype(jnp.float32) + scale_for_norm(proj, attn_gain)).astype(jnp.bfloat16)
    widened = lax.optimization_barrier(hstate).astype(jnp.float32)
    normed = scale_for_norm(widened, pre_gain).astype(jnp.bfloat16)
    gate = jnp.dot(normed, w_gate, preferred_element_type=jnp.float32)
    up = jnp.dot(normed, w_up, preferred_element_type=jnp.float32)
    hidden = (jax.nn.gelu(gate, approximate=True) * up).astype(jnp.bfloat16)
    down = jnp.dot(hidden, w_down, preferred_element_type=jnp.float32)
    out = (widened + scale_for_norm(down, post_gain)).astype(jnp.bfloat16)
    return out.reshape(REQUEST_COUNT, DECODE_STEPS, D)
```

```python
import functools
import jax
import jax.numpy as jnp
from jax import lax
from jax.experimental import pallas as pl
from jax.experimental.pallas import tpu as pltpu
from jax.sharding import PartitionSpec as P

MESH = pl.DeviceIdType.MESH
ANY = pl.BlockSpec(memory_space=pl.ANY)
VMEM = pl.BlockSpec(memory_space=pltpu.VMEM)
F32 = jnp.float32
BF16 = jnp.bfloat16
eps = 1e-06
theta = 1000000.0
LOW = -3e38
SAFE = -1.5e38


def scale_for_norm(rows, gain):
    mean_square = jnp.mean(rows * rows, axis=-1, keepdims=True)
    return rows * lax.rsqrt(mean_square + eps) * gain


def nt(a, b):
    return lax.dot_general(a, b, (((1,), (1,)), ((), ())), preferred_element_type=F32)


def nn(a, b):
    return jnp.dot(a, b, preferred_element_type=F32)


def attention(q_ref, fk_ref, fv_ref, gain_ref, cs_ref, info_ref, pk, pv, tk, tv, num_ref, st_ref,
              kb, vb, tkb, tvb, sems):
    requests, steps, _ = q_ref.shape
    heads, groups, block, hd = kb.shape
    tail_block = tkb.shape[2]
    rows = requests * 2 * steps
    per = 2 * steps
    chunk = min(4, requests)
    seq = lax.axis_index("seq")
    copies = []
    for k in range(heads):
        cols = pl.ds(k * hd, hd)
        some = [
            pltpu.make_async_copy(pk.at[:, :, cols], kb.at[k], sems.at[k, 0]),
            pltpu.make_async_copy(tk.at[:, :, cols], tkb.at[k], sems.at[k, 1]),
            pltpu.make_async_copy(pv.at[:, :, cols], vb.at[k], sems.at[k, 2]),
            pltpu.make_async_copy(tv.at[:, :, cols], tvb.at[k], sems.at[k, 3]),
        ]
        for copy in some:
            copy.start()
        copies.append(some)
    cosine, sine = cs_ref[0], cs_ref[1]
    first = info_ref[:, 0:1] == 0
    prompt_end = info_ref[:, 1:2]
    tail_end = info_ref[:, 2:3]
    slot = seq * block + lax.broadcasted_iota(jnp.int32, (rows, block), 1)
    prompt_ok = slot < prompt_end
    width = chunk * tail_block
    row = lax.broadcasted_iota(jnp.int32, (rows, width), 0)
    col = lax.broadcasted_iota(jnp.int32, (rows, width), 1)
    tail_ok = ((row // per) % chunk == col // tail_block) & (
        seq * tail_block + col % tail_block < tail_end
    )
    row = lax.broadcasted_iota(jnp.int32, (rows, rows), 0)
    col = lax.broadcasted_iota(jnp.int32, (rows, rows), 1)
    own_ok = (
        (row // per == col // per) & (col % per <= row % steps) & (row // per == seq)
    )
    half = hd // 2

    def rotate(v):
        a, b = v[:, :half], v[:, half:]
        return jnp.concatenate([a * cosine - b * sine, b * cosine + a * sine], axis=1)

    def doubled(a, b):
        return jnp.concatenate([a.astype(F32), b.astype(F32)], axis=1).reshape(rows, hd)

    lane = lax.broadcasted_iota(jnp.int32, (rows, 128), 1)
    stats = jnp.zeros((rows, 128), F32)
    for k in range(heads):
        q = doubled(q_ref[:, :, 2 * k * hd:(2 * k + 1) * hd], q_ref[:, :, (2 * k + 1) * hd:(2 * k + 2) * hd])
        q = (rotate(scale_for_norm(q, gain_ref[...])) * hd ** (-0.5)).astype(BF16)
        fk = fk_ref[:, :, k * hd:(k + 1) * hd]
        own_key = rotate(scale_for_norm(doubled(fk, fk), 1.0)).astype(BF16)
        fv = fv_ref[:, :, k * hd:(k + 1) * hd]
        own_value = doubled(fv, fv).astype(BF16)
        copies[k][0].wait()
        s = jnp.where(first, nt(q, kb[k, 0]), nt(q, kb[k, 1]))
        s = jnp.where(prompt_ok, s, LOW)
        copies[k][1].wait()
        t = jnp.concatenate(
            [
                nt(q[c * chunk * per:(c + 1) * chunk * per], tkb[k, c * chunk:(c + 1) * chunk].reshape(width, hd))
                for c in range(requests // chunk)
            ],
            axis=0,
        )
        t = jnp.where(tail_ok, t, LOW)
        o = jnp.where(own_ok, nt(q, own_key), LOW)
        peak = jnp.maximum(
            jnp.maximum(jnp.max(s, axis=1, keepdims=True), jnp.max(t, axis=1, keepdims=True)),
            jnp.max(o, axis=1, keepdims=True),
        )
        peak = jnp.maximum(peak, SAFE)
        s = jnp.exp(s - peak)
        t = jnp.exp(t - peak)
        o = jnp.exp(o - peak)
        total = (
            jnp.sum(s, axis=1, keepdims=True) + jnp.sum(t, axis=1, keepdims=True) + jnp.sum(o, axis=1, keepdims=True)
        )
        stats = jnp.where(lane == k, peak, jnp.where(lane == heads + k, total, stats))
        t = t.astype(BF16)
        num = nn(o.astype(BF16), own_value)
        copies[k][2].wait()
        num += nn(jnp.where(first, s, 0.0).astype(BF16), vb[k, 0])
        num += nn(jnp.where(first, 0.0, s).astype(BF16), vb[k, 1])
        copies[k][3].wait()
        num += jnp.concatenate(
            [
                nn(t[c * chunk * per:(c + 1) * chunk * per], tvb[k, c * chunk:(c + 1) * chunk].reshape(width, hd))
                for c in range(requests // chunk)
            ],
            axis=0,
        )
        num_ref[:, k] = num.reshape(requests, per, hd).astype(BF16)
    st_ref[...] = stats.reshape(requests, per, 128)


def exchange(n, parts, num, st, resid, wo_h, wg_h, wu_h, wd_h, again, pgain, qgain, out_ref,
             an, ast, own_num, own_st, res, wo, wg, wu, wgu, wd, nb, x, p, rsib, s,
             r2a, r2b, r2c, ta, tb, tc, r1a, r1b, r1c, dn, hst,
             lsem, asend, arecv, sbs, sbr, s1s, s1r, lns, lnr, xs, xr, p3s, p3r, r2s, r2r, r1s, r1r):
    seq, req = lax.axis_index("seq"), lax.axis_index("req")
    me = (seq // n, seq % n, req // 2)
    c = req % 2
    heads = num.shape[1]
    steps = out_ref.shape[1]
    d = out_ref.shape[2]
    half = d // 2
    ff = wg.shape[1]
    r2, t, r1 = (r2a, r2b, r2c), (ta, tb, tc), (r1a, r1b, r1c)

    def device(zxy, core):
        return (zxy[0] * n + zxy[1], zxy[2] * 2 + core)

    def moved(offset):
        return tuple((m + o) % n for m, o in zip(me, offset))

    sibling = device(me, 1 - c)
    line_axis = (2, 0, 1)
    plane_axes = ((0, 1), (1, 2), (0, 2))

    def offset_of(part, dl, da, db):
        o = [0, 0, 0]
        o[line_axis[part]] = dl
        o[plane_axes[part][0]] = da
        o[plane_axes[part][1]] = db
        return tuple(o)

    def line_slice(ref, part, value, cols):
        index = [slice(None)] * 3
        index[line_axis[part]] = value
        return ref.at[(*index, slice(None), cols)]

    plane = [(i, j) for i in range(n) for j in range(n) if (i, j) != (0, 0)]
    partners = [
        (i, j, k) for i in range(n) for j in range(n) for k in range(n)
        if 0 < (i > 0) + (j > 0) + (k > 0) < 3
    ]

    loads = [
        pltpu.make_async_copy(num.at[seq], own_num, lsem.at[0]),
        pltpu.make_async_copy(st.at[seq], own_st, lsem.at[1]),
        pltpu.make_async_copy(resid.at[seq], res, lsem.at[2]),
        pltpu.make_async_copy(wg_h, wg, lsem.at[3]),
        pltpu.make_async_copy(wu_h, wu, lsem.at[4]),
        pltpu.make_async_copy(wd_h, wd.at[pl.ds(0, ff)], lsem.at[5]),
        pltpu.make_async_copy(wo_h, wo, lsem.at[6]),
    ]
    barrier = pltpu.get_barrier_semaphore()
    for o in partners:
        pl.semaphore_signal(barrier, inc=1, device_id=device(moved(o), c), device_id_type=MESH)
    pl.semaphore_signal(barrier, inc=1, device_id=sibling, device_id_type=MESH)
    pl.semaphore_wait(barrier, len(partners) + 1)

    def remote(src, dst, send, recv, where):
        copy = pltpu.make_async_remote_copy(
            src_ref=src, dst_ref=dst, send_sem=send, recv_sem=recv, device_id=where, device_id_type=MESH
        )
        copy.start()
        return copy

    sent = []
    attn = []
    for index, (i, j) in enumerate(plane):
        to = moved((i, j, 0))
        dest = to[0] * n + to[1]
        attn.append(remote(num.at[dest], an.at[index], asend.at[0, index], arecv.at[0, index], device(to, c)))
        attn.append(remote(st.at[dest], ast.at[index], asend.at[1, index], arecv.at[1, index], device(to, c)))
    sent += attn
    for copy in loads:
        copy.start()
    loads[3].wait()
    wgu[:, 0:128] = jnp.concatenate([wg[...], jnp.zeros((d, 128 - ff), BF16)], axis=1)
    loads[4].wait()
    wgu[:, 128:256] = jnp.concatenate([wu[...], jnp.zeros((d, 128 - ff), BF16)], axis=1)
    loads[5].wait()
    wd[ff:128, :] = jnp.zeros((128 - ff, d), BF16)
    for copy in loads[:3]:
        copy.wait()
    for copy in attn:
        copy.wait_recv()
    st_all = [own_st[...]] + [ast[i] for i in range(len(plane))]
    peak = functools.reduce(jnp.maximum, st_all)
    shrink = [jnp.exp(v[:, :heads] - peak[:, :heads]) for v in st_all]
    total = sum(w * v[:, heads:2 * heads] for w, v in zip(shrink, st_all))
    loads[6].wait()
    proj = None
    hd = num.shape[3]
    for k in range(heads):
        mixed = own_num[k].astype(F32) * shrink[0][:, k:k + 1]
        for i in range(len(plane)):
            mixed += an[i, k].astype(F32) * shrink[i + 1][:, k:k + 1]
        mixed = (mixed / total[:, k:k + 1]).astype(BF16)
        one = nn(mixed, wo[2 * k * hd:(2 * k + 1) * hd, :])
        two = nn(mixed, wo[(2 * k + 1) * hd:(2 * k + 2) * hd, :])
        term = one[:steps] + two[steps:]
        proj = term if proj is None else proj + term
    hstate = (res[...].astype(F32) + scale_for_norm(proj, again[...])).astype(BF16)
    hst[...] = hstate
    nb[c] = scale_for_norm(hstate.astype(F32), pgain[...]).astype(BF16)
    copy = remote(nb.at[c], nb.at[c], sbs.at[0], sbr.at[0], sibling)
    sent.append(copy)
    copy.wait_recv()
    both = jnp.concatenate([nb[0].astype(F32), nb[1].astype(F32)], axis=0).astype(BF16)
    x[(c, *me)] = jnp.where(c == 0, both[:, :half], both[:, half:])

    mine = x.at[c]
    first = []
    for part, (at, size) in enumerate(parts):
        cols = pl.ds(at, size)
        block = mine.at[(*me, slice(None), cols)]
        row = []
        for index, (i, j) in enumerate(plane):
            where = device(moved(offset_of(part, 0, i, j)), c)
            row.append(remote(block, block, s1s.at[part, index], s1r.at[part, index], where))
        first.append(row)
        sent += row
    lines, siblings = [], []
    for part, (at, size) in enumerate(parts):
        cols = pl.ds(at, size)
        for copy in first[part]:
            copy.wait_recv()
        piece = line_slice(mine, part, me[line_axis[part]], cols)
        row = []
        for dl in range(1, n):
            where = device(moved(offset_of(part, dl, 0, 0)), c)
            row.append(remote(piece, piece, lns.at[part, dl - 1], lnr.at[part, dl - 1], where))
        siblings.append(remote(piece, piece, xs.at[part, 0], xr.at[part, 0], sibling))
        lines.append(row)
        sent += row
    for dl in sorted(range(1, n), key=lambda v: min(v, n - v)):
        for part, (at, size) in enumerate(parts):
            lines[part][dl - 1].wait_recv()
            source = (me[line_axis[part]] - dl + n) % n
            piece = line_slice(mine, part, source, pl.ds(at, size))
            siblings.append(remote(piece, piece, xs.at[part, dl], xr.at[part, dl], sibling))
    sent += siblings
    for copy in siblings:
        copy.wait_recv()

    count = n * n * 8
    third = []
    for z in range(n):
        gu = nn(x[0, z].reshape(count, half), wgu[:half]) + nn(x[1, z].reshape(count, half), wgu[half:])
        hidden = (jax.nn.gelu(gu[:, :128], approximate=True) * gu[:, 128:]).astype(BF16)
        down = nn(hidden, wd[...])
        p[0, z] = down[:, :half].astype(BF16).reshape(n, n, 8, half)
        p[1, z] = down[:, half:].astype(BF16).reshape(n, n, 8, half)
        third.append(remote(p.at[1 - c, z], rsib.at[z], p3s.at[z], p3r.at[z], sibling))
    sent += third
    for z in range(n):
        third[z].wait_recv()
        s[z] = (p[c, z].astype(F32) + rsib[z].astype(F32)).astype(BF16)
    second = []
    for part, (at, size) in enumerate(parts):
        row = []
        for dl in range(1, n):
            to = moved(offset_of(part, dl, 0, 0))
            piece = line_slice(s, part, to[line_axis[part]], pl.ds(at, size))
            row.append(remote(piece, r2[part].at[dl - 1], r2s.at[part, dl - 1], r2r.at[part, dl - 1], device(to, c)))
        second.append(row)
        sent += row
    last = []
    for part, (at, size) in enumerate(parts):
        for copy in second[part]:
            copy.wait_recv()
        own = line_slice(s, part, me[line_axis[part]], pl.ds(at, size))
        total = own[...].astype(F32)
        for dl in range(1, n):
            total += r2[part][dl - 1].astype(F32)
        t[part][...] = total.astype(BF16)
        row = []
        for index, (i, j) in enumerate(plane):
            to = moved(offset_of(part, 0, i, j))
            a, b = (to[v] for v in plane_axes[part])
            row.append(remote(t[part].at[a, b], r1[part].at[index], r1s.at[part, index], r1r.at[part, index],
                              device(to, c)))
        last.append(row)
        sent += row
    for part, (at, size) in enumerate(parts):
        for copy in last[part]:
            copy.wait_recv()
        a, b = (me[v] for v in plane_axes[part])
        total = t[part][a, b].astype(F32)
        for index in range(len(plane)):
            total += r1[part][index].astype(F32)
        dn[c, :, at:at + size] = total
    copy = remote(dn.at[c], dn.at[c], sbs.at[1], sbr.at[1], sibling)
    sent.append(copy)
    copy.wait_recv()
    down = jnp.concatenate([dn[0], dn[1]], axis=1)
    down = jnp.where(c == 0, down[:steps], down[steps:])
    out_ref[0] = (hst[...].astype(F32) + scale_for_norm(down, qgain[...])).astype(BF16)
    for copy in sent:
        copy.wait_send()


def shards(n, q_new, fresh_keys, fresh_values, q_gain, prompt_key_cache, prompt_value_cache, tail_key_cache,
           tail_value_cache, group_of, prefix_len, tail_len, resid, w_out, attn_gain, pre_gain, post_gain,
           w_gate, w_up, w_down):
    requests, steps, query_width = q_new.shape
    hd = q_gain.shape[0]
    heads = fresh_keys.shape[2] // hd
    groups, block, _ = prompt_key_cache.shape
    tail_block = tail_key_cache.shape[1]
    d = resid.shape[2]
    half = d // 2
    ff = w_gate.shape[1]
    rows = requests * 2 * steps
    per = 2 * steps
    member = group_of[:, None] == jnp.arange(groups, dtype=jnp.int32)[None, :]
    prompt_end = jnp.sum(jnp.where(member, prefix_len[None, :], 0), axis=1)
    info = jnp.stack([group_of, prompt_end, tail_len, prompt_end + tail_len], axis=1)
    info = jnp.broadcast_to(info[:, None, :], (requests, per, 4)).reshape(rows, 4)
    step = jnp.arange(rows, dtype=jnp.int32) % steps
    positions = (info[:, 3] + step).astype(F32)
    freq = theta ** (-(jnp.arange(hd // 2, dtype=F32) * 2.0 / hd))
    angle = positions[:, None] * freq
    cs = jnp.stack([jnp.cos(angle), jnp.sin(angle)])
    num, st = pl.pallas_call(
        attention,
        out_shape=(
            jax.ShapeDtypeStruct((requests, heads, per, hd), BF16),
            jax.ShapeDtypeStruct((requests, per, 128), F32),
        ),
        in_specs=[VMEM] * 6 + [ANY] * 4,
        out_specs=(VMEM, VMEM),
        scratch_shapes=[
            pltpu.VMEM((heads, groups, block, hd), BF16),
            pltpu.VMEM((heads, groups, block, hd), BF16),
            pltpu.VMEM((heads, requests, tail_block, hd), BF16),
            pltpu.VMEM((heads, requests, tail_block, hd), BF16),
            pltpu.SemaphoreType.DMA((heads, 4)),
        ],
        name="attention",
    )(q_new, fresh_keys, fresh_values, q_gain[None, :], cs, info,
      prompt_key_cache, prompt_value_cache, tail_key_cache, tail_value_cache)
    tiles = half // 128
    sizes = [128 * ((tiles + 2 - i) // 3) for i in range(3)]
    parts = [(sum(sizes[:i]), sizes[i]) for i in range(3)]
    np_ = n * n - 1
    dma = pltpu.SemaphoreType.DMA
    scratch = [
        pltpu.VMEM((np_, heads, per, hd), BF16),
        pltpu.VMEM((np_, per, 128), F32),
        pltpu.VMEM((heads, per, hd), BF16),
        pltpu.VMEM((per, 128), F32),
        pltpu.VMEM((steps, d), BF16),
        pltpu.VMEM(w_out.shape, BF16),
        pltpu.VMEM((d, ff), BF16),
        pltpu.VMEM((d, ff), BF16),
        pltpu.VMEM((d, 256), BF16),
        pltpu.VMEM((128, d), BF16),
        pltpu.VMEM((2, steps, d), BF16),
        pltpu.VMEM((2, n, n, n, 8, half), BF16),
        pltpu.VMEM((2, n, n, n, 8, half), BF16),
        pltpu.VMEM((n, n, n, 8, half), BF16),
        pltpu.VMEM((n, n, n, 8, half), BF16),
    ]
    scratch += [pltpu.VMEM((n - 1, n, n, 8, size), BF16) for size in sizes]
    scratch += [pltpu.VMEM((n, n, 8, size), BF16) for size in sizes]
    scratch += [pltpu.VMEM((np_, 8, size), BF16) for size in sizes]
    scratch += [
        pltpu.VMEM((2, 8, half), F32),
        pltpu.VMEM((steps, d), BF16),
        dma((7,)), dma((2, np_)), dma((2, np_)), dma((2,)), dma((2,)), dma((3, np_)), dma((3, np_)),
        dma((3, n - 1)), dma((3, n - 1)), dma((3, n)), dma((3, n)), dma((n,)), dma((n,)),
        dma((3, n - 1)), dma((3, n - 1)), dma((3, np_)), dma((3, np_)),
    ]
    return pl.pallas_call(
        functools.partial(exchange, n, parts),
        out_shape=jax.ShapeDtypeStruct((1, steps, d), BF16),
        in_specs=[ANY] * 2 + [ANY] * 5 + [VMEM] * 3,
        out_specs=VMEM,
        scratch_shapes=scratch,
        compiler_params=pltpu.CompilerParams(collective_id=0, has_side_effects=True),
        name="exchange",
    )(num, st, resid, w_out, w_gate, w_up, w_down, attn_gain[None, :], pre_gain[None, :], post_gain[None, :])


def solution(mesh):
    in_specs = (
        P("req", None, None), P("req", None, None), P("req", None, None), P(),
        P("req", "seq", None), P("req", "seq", None), P("req", "seq", None), P("req", "seq", None),
        P("req"), P("req"), P("req"), P("req", None, None), P(), P(), P(), P(),
        P(None, ("seq", "req")), P(None, ("seq", "req")), P(("seq", "req"), None),
    )
    n = mesh.shape["req"] // 2
    return jax.shard_map(
        functools.partial(shards, n), mesh=mesh, in_specs=in_specs,
        out_specs=P(("req", "seq"), None, None), check_vma=False,
    )
```

```python
import functools
import jax
import jax.numpy as jnp
from jax import lax
from jax.experimental import pallas as pl
from jax.experimental.pallas import tpu as pltpu
from jax.sharding import PartitionSpec as P

MESH = pl.DeviceIdType.MESH
ANY = pl.BlockSpec(memory_space=pl.ANY)
SMEM = pl.BlockSpec(memory_space=pltpu.SMEM)
VMEM = pl.BlockSpec(memory_space=pltpu.VMEM)
F32 = jnp.float32
BF16 = jnp.bfloat16
eps = 1e-06
theta = 1000000.0
LOW = -3e38
SAFE = -1.5e38


def scale_for_norm(rows, gain):
    mean_square = jnp.mean(rows * rows, axis=-1, keepdims=True)
    return rows * lax.rsqrt(mean_square + eps) * gain


def nt(a, b):
    return lax.dot_general(a, b, (((1,), (1,)), ((), ())), preferred_element_type=F32)


def nn(a, b):
    return jnp.dot(a, b, preferred_element_type=F32)


def attention(q_ref, fk_ref, fv_ref, gain_ref, freq_ref, group_ref, prefix_ref, tail_ref, pk, pv, tk, tv, num_ref, st_ref,
              kb, vb, tkb, tvb, sems):
    requests, steps, _ = q_ref.shape
    heads, groups, block, hd = kb.shape
    tail_block = tkb.shape[2]
    rows = requests * 2 * steps
    per = 2 * steps
    chunk = min(4, requests)
    seq = lax.axis_index("seq")
    copies = []
    for k in range(heads):
        cols = pl.ds(k * hd, hd)
        some = [
            pltpu.make_async_copy(pk.at[:, :, cols], kb.at[k], sems.at[k, 0]),
            pltpu.make_async_copy(tk.at[:, :, cols], tkb.at[k], sems.at[k, 1]),
            pltpu.make_async_copy(pv.at[:, :, cols], vb.at[k], sems.at[k, 2]),
            pltpu.make_async_copy(tv.at[:, :, cols], tvb.at[k], sems.at[k, 3]),
        ]
        for copy in some:
            copy.start()
        copies.append(some)
    ends, tails, members = [], [], []
    for r in range(requests):
        group = group_ref[r]
        end = prefix_ref[0]
        for g in range(1, groups):
            end = jnp.where(group == g, prefix_ref[g], end)
        ends.append(jnp.full((per, 128), end, jnp.int32))
        tails.append(jnp.full((per, 128), tail_ref[r], jnp.int32))
        members.append(jnp.full((per, 128), group, jnp.int32))
    ends, tails, members = (jnp.concatenate(v, axis=0) for v in (ends, tails, members))
    step = lax.broadcasted_iota(jnp.int32, (rows, 128), 0) % steps
    angle = (ends + tails + step).astype(F32) * freq_ref[...].reshape(1, 128)
    cosine, sine = jnp.cos(angle), jnp.sin(angle)
    first = members[:, 0:1] == 0
    prompt_end = ends[:, 0:1]
    tail_end = tails[:, 0:1]
    slot = seq * block + lax.broadcasted_iota(jnp.int32, (rows, block), 1)
    prompt_ok = slot < prompt_end
    width = chunk * tail_block
    row = lax.broadcasted_iota(jnp.int32, (rows, width), 0)
    col = lax.broadcasted_iota(jnp.int32, (rows, width), 1)
    tail_ok = ((row // per) % chunk == col // tail_block) & (
        seq * tail_block + col % tail_block < tail_end
    )
    row = lax.broadcasted_iota(jnp.int32, (rows, rows), 0)
    col = lax.broadcasted_iota(jnp.int32, (rows, rows), 1)
    own_ok = (
        (row // per == col // per) & (col % per <= row % steps) & (row // per == seq)
    )
    half = hd // 2

    def rotate(v):
        a, b = v[:, :half], v[:, half:]
        return jnp.concatenate([a * cosine - b * sine, b * cosine + a * sine], axis=1)

    def doubled(a, b):
        return jnp.concatenate([a.astype(F32), b.astype(F32)], axis=1).reshape(rows, hd)

    lane = lax.broadcasted_iota(jnp.int32, (rows, 128), 1)
    stats = jnp.zeros((rows, 128), F32)
    for k in range(heads):
        q = doubled(q_ref[:, :, 2 * k * hd:(2 * k + 1) * hd], q_ref[:, :, (2 * k + 1) * hd:(2 * k + 2) * hd])
        q = (rotate(scale_for_norm(q, gain_ref[...].reshape(1, hd))) * hd ** (-0.5)).astype(BF16)
        fk = fk_ref[:, :, k * hd:(k + 1) * hd]
        own_key = rotate(scale_for_norm(doubled(fk, fk), 1.0)).astype(BF16)
        fv = fv_ref[:, :, k * hd:(k + 1) * hd]
        own_value = doubled(fv, fv).astype(BF16)
        copies[k][0].wait()
        s = jnp.where(first, nt(q, kb[k, 0]), nt(q, kb[k, 1]))
        s = jnp.where(prompt_ok, s, LOW)
        copies[k][1].wait()
        t = jnp.concatenate(
            [
                nt(q[c * chunk * per:(c + 1) * chunk * per], tkb[k, c * chunk:(c + 1) * chunk].reshape(width, hd))
                for c in range(requests // chunk)
            ],
            axis=0,
        )
        t = jnp.where(tail_ok, t, LOW)
        o = jnp.where(own_ok, nt(q, own_key), LOW)
        peak = jnp.maximum(
            jnp.maximum(jnp.max(s, axis=1, keepdims=True), jnp.max(t, axis=1, keepdims=True)),
            jnp.max(o, axis=1, keepdims=True),
        )
        peak = jnp.maximum(peak, SAFE)
        s = jnp.exp(s - peak)
        t = jnp.exp(t - peak)
        o = jnp.exp(o - peak)
        total = (
            jnp.sum(s, axis=1, keepdims=True) + jnp.sum(t, axis=1, keepdims=True) + jnp.sum(o, axis=1, keepdims=True)
        )
        stats = jnp.where(lane == k, peak, jnp.where(lane == heads + k, total, stats))
        t = t.astype(BF16)
        num = nn(o.astype(BF16), own_value)
        copies[k][2].wait()
        num += nn(jnp.where(first, s, 0.0).astype(BF16), vb[k, 0])
        num += nn(jnp.where(first, 0.0, s).astype(BF16), vb[k, 1])
        copies[k][3].wait()
        num += jnp.concatenate(
            [
                nn(t[c * chunk * per:(c + 1) * chunk * per], tvb[k, c * chunk:(c + 1) * chunk].reshape(width, hd))
                for c in range(requests // chunk)
            ],
            axis=0,
        )
        num_ref[:, k] = num.reshape(requests, per, hd).astype(BF16)
    st_ref[...] = stats.reshape(requests, per, 128)


def exchange(n, parts, num, st, resid, wo_h, wg_h, wu_h, wd_h, again, pgain, qgain, out_ref,
             an, ast, own_num, own_st, res, wo, wgu, wd, nb, x, p, rsib, s,
             r2a, r2b, r2c, ta, tb, tc, r1a, r1b, r1c, dn, hst,
             lsem, asend, arecv, sbs, sbr, s1s, s1r, lns, lnr, xs, xr, p3s, p3r, r2s, r2r, r1s, r1r):
    seq, req = lax.axis_index("seq"), lax.axis_index("req")
    me = (seq // n, seq % n, req // 2)
    c = req % 2
    heads = num.shape[1]
    steps = out_ref.shape[1]
    d = out_ref.shape[2]
    half = d // 2
    ff = wd_h.shape[0]
    r2, t, r1 = (r2a, r2b, r2c), (ta, tb, tc), (r1a, r1b, r1c)

    def device(zxy, core):
        return (zxy[0] * n + zxy[1], zxy[2] * 2 + core)

    def moved(offset):
        return tuple((m + o) % n for m, o in zip(me, offset))

    sibling = device(me, 1 - c)
    line_axis = (2, 0, 1)
    plane_axes = ((0, 1), (1, 2), (0, 2))

    def offset_of(part, dl, da, db):
        o = [0, 0, 0]
        o[line_axis[part]] = dl
        o[plane_axes[part][0]] = da
        o[plane_axes[part][1]] = db
        return tuple(o)

    def line_slice(ref, part, value, cols):
        index = [slice(None)] * 3
        index[line_axis[part]] = value
        return ref.at[(*index, slice(None), cols)]

    plane = [(i, j) for i in range(n) for j in range(n) if (i, j) != (0, 0)]
    partners = [
        (i, j, k) for i in range(n) for j in range(n) for k in range(n)
        if 0 < (i > 0) + (j > 0) + (k > 0) < 3
    ]

    loads = [
        pltpu.make_async_copy(num.at[seq], own_num, lsem.at[0]),
        pltpu.make_async_copy(st.at[seq], own_st, lsem.at[1]),
        pltpu.make_async_copy(resid.at[seq], res, lsem.at[2]),
        pltpu.make_async_copy(wg_h, wgu.at[pl.ds(0, ff)], lsem.at[3]),
        pltpu.make_async_copy(wu_h, wgu.at[pl.ds(128, ff)], lsem.at[4]),
        pltpu.make_async_copy(wd_h, wd.at[pl.ds(0, ff)], lsem.at[5]),
        pltpu.make_async_copy(wo_h, wo, lsem.at[6]),
    ]
    barrier = pltpu.get_barrier_semaphore()
    for o in partners:
        pl.semaphore_signal(barrier, inc=1, device_id=device(moved(o), c), device_id_type=MESH)
    pl.semaphore_signal(barrier, inc=1, device_id=sibling, device_id_type=MESH)
    pl.semaphore_wait(barrier, len(partners) + 1)

    def remote(src, dst, send, recv, where):
        copy = pltpu.make_async_remote_copy(
            src_ref=src, dst_ref=dst, send_sem=send, recv_sem=recv, device_id=where, device_id_type=MESH
        )
        copy.start()
        return copy

    sent = []
    attn = []
    for index, (i, j) in enumerate(plane):
        to = moved((i, j, 0))
        dest = to[0] * n + to[1]
        attn.append(remote(num.at[dest], an.at[index], asend.at[0, index], arecv.at[0, index], device(to, c)))
        attn.append(remote(st.at[dest], ast.at[index], asend.at[1, index], arecv.at[1, index], device(to, c)))
    sent += attn
    for copy in loads:
        copy.start()
    wgu[ff:128, :] = jnp.zeros((128 - ff, d), BF16)
    wgu[128 + ff:256, :] = jnp.zeros((128 - ff, d), BF16)
    wd[ff:128, :] = jnp.zeros((128 - ff, d), BF16)
    for copy in loads[:6]:
        copy.wait()
    for copy in attn:
        copy.wait_recv()
    st_all = [own_st[...]] + [ast[i] for i in range(len(plane))]
    peak = functools.reduce(jnp.maximum, st_all)
    shrink = [jnp.exp(v[:, :heads] - peak[:, :heads]) for v in st_all]
    total = sum(w * v[:, heads:2 * heads] for w, v in zip(shrink, st_all))
    loads[6].wait()
    proj = None
    hd = num.shape[3]
    for k in range(heads):
        mixed = own_num[k].astype(F32) * shrink[0][:, k:k + 1]
        for i in range(len(plane)):
            mixed += an[i, k].astype(F32) * shrink[i + 1][:, k:k + 1]
        mixed = (mixed / total[:, k:k + 1]).astype(BF16)
        one = nn(mixed, wo[2 * k * hd:(2 * k + 1) * hd, :])
        two = nn(mixed, wo[(2 * k + 1) * hd:(2 * k + 2) * hd, :])
        term = one[:steps] + two[steps:]
        proj = term if proj is None else proj + term
    hstate = (res[...].astype(F32) + scale_for_norm(proj, again[...].reshape(1, d))).astype(BF16)
    hst[...] = hstate
    nb[c] = scale_for_norm(hstate.astype(F32), pgain[...].reshape(1, d)).astype(BF16)
    copy = remote(nb.at[c], nb.at[c], sbs.at[0], sbr.at[0], sibling)
    sent.append(copy)
    copy.wait_recv()
    both = jnp.concatenate([nb[0].astype(F32), nb[1].astype(F32)], axis=0).astype(BF16)
    x[(c, *me)] = jnp.where(c == 0, both[:, :half], both[:, half:])

    mine = x.at[c]
    first = []
    for part, (at, size) in enumerate(parts):
        cols = pl.ds(at, size)
        block = mine.at[(*me, slice(None), cols)]
        row = []
        for index, (i, j) in enumerate(plane):
            where = device(moved(offset_of(part, 0, i, j)), c)
            row.append(remote(block, block, s1s.at[part, index], s1r.at[part, index], where))
        first.append(row)
        sent += row
    lines, siblings = [], []
    for part, (at, size) in enumerate(parts):
        cols = pl.ds(at, size)
        for copy in first[part]:
            copy.wait_recv()
        piece = line_slice(mine, part, me[line_axis[part]], cols)
        row = []
        for dl in range(1, n):
            where = device(moved(offset_of(part, dl, 0, 0)), c)
            row.append(remote(piece, piece, lns.at[part, dl - 1], lnr.at[part, dl - 1], where))
        siblings.append(remote(piece, piece, xs.at[part, 0], xr.at[part, 0], sibling))
        lines.append(row)
        sent += row
    for dl in sorted(range(1, n), key=lambda v: min(v, n - v)):
        for part, (at, size) in enumerate(parts):
            lines[part][dl - 1].wait_recv()
            source = (me[line_axis[part]] - dl + n) % n
            piece = line_slice(mine, part, source, pl.ds(at, size))
            siblings.append(remote(piece, piece, xs.at[part, dl], xr.at[part, dl], sibling))
    sent += siblings
    for copy in siblings:
        copy.wait_recv()

    count = n * n * 8
    third = []
    for z in range(n):
        gu = nt(x[0, z].reshape(count, half), wgu[:, :half]) + nt(x[1, z].reshape(count, half), wgu[:, half:])
        hidden = (jax.nn.gelu(gu[:, :128], approximate=True) * gu[:, 128:]).astype(BF16)
        down = nn(hidden, wd[...])
        p[0, z] = down[:, :half].astype(BF16).reshape(n, n, 8, half)
        p[1, z] = down[:, half:].astype(BF16).reshape(n, n, 8, half)
        third.append(remote(p.at[1 - c, z], rsib.at[z], p3s.at[z], p3r.at[z], sibling))
    sent += third
    for z in range(n):
        third[z].wait_recv()
        s[z] = (p[c, z].astype(F32) + rsib[z].astype(F32)).astype(BF16)
    second = []
    for part, (at, size) in enumerate(parts):
        row = []
        for dl in range(1, n):
            to = moved(offset_of(part, dl, 0, 0))
            piece = line_slice(s, part, to[line_axis[part]], pl.ds(at, size))
            row.append(remote(piece, r2[part].at[dl - 1], r2s.at[part, dl - 1], r2r.at[part, dl - 1], device(to, c)))
        second.append(row)
        sent += row
    last = []
    for part, (at, size) in enumerate(parts):
        for copy in second[part]:
            copy.wait_recv()
        own = line_slice(s, part, me[line_axis[part]], pl.ds(at, size))
        total = own[...].astype(F32)
        for dl in range(1, n):
            total += r2[part][dl - 1].astype(F32)
        t[part][...] = total.astype(BF16)
        row = []
        for index, (i, j) in enumerate(plane):
            to = moved(offset_of(part, 0, i, j))
            a, b = (to[v] for v in plane_axes[part])
            row.append(remote(t[part].at[a, b], r1[part].at[index], r1s.at[part, index], r1r.at[part, index],
                              device(to, c)))
        last.append(row)
        sent += row
    for part, (at, size) in enumerate(parts):
        for copy in last[part]:
            copy.wait_recv()
        a, b = (me[v] for v in plane_axes[part])
        total = t[part][a, b].astype(F32)
        for index in range(len(plane)):
            total += r1[part][index].astype(F32)
        dn[c, :, at:at + size] = total
    copy = remote(dn.at[c], dn.at[c], sbs.at[1], sbr.at[1], sibling)
    sent.append(copy)
    copy.wait_recv()
    down = jnp.concatenate([dn[0], dn[1]], axis=1)
    down = jnp.where(c == 0, down[:steps], down[steps:])
    out_ref[0] = hst[...].astype(F32) + scale_for_norm(down, qgain[...].reshape(1, d))
    for copy in sent:
        copy.wait_send()


def shards(n, q_new, fresh_keys, fresh_values, q_gain, prompt_key_cache, prompt_value_cache, tail_key_cache,
           tail_value_cache, group_of, prefix_len, tail_len, resid, w_out, attn_gain, pre_gain, post_gain,
           w_gate, w_up, w_down):
    requests, steps, query_width = q_new.shape
    hd = q_gain.shape[0]
    heads = fresh_keys.shape[2] // hd
    groups, block, _ = prompt_key_cache.shape
    tail_block = tail_key_cache.shape[1]
    d = resid.shape[2]
    half = d // 2
    ff = w_gate.shape[1]
    rows = requests * 2 * steps
    per = 2 * steps
    freq = theta ** (-(jnp.arange(hd // 2, dtype=F32) * 2.0 / hd))
    num, st = pl.pallas_call(
        attention,
        out_shape=(
            jax.ShapeDtypeStruct((requests, heads, per, hd), BF16),
            jax.ShapeDtypeStruct((requests, per, 128), F32),
        ),
        in_specs=[VMEM] * 5 + [SMEM] * 3 + [ANY] * 4,
        out_specs=(VMEM, VMEM),
        scratch_shapes=[
            pltpu.VMEM((heads, groups, block, hd), BF16),
            pltpu.VMEM((heads, groups, block, hd), BF16),
            pltpu.VMEM((heads, requests, tail_block, hd), BF16),
            pltpu.VMEM((heads, requests, tail_block, hd), BF16),
            pltpu.SemaphoreType.DMA((heads, 4)),
        ],
        name="attention",
    )(q_new, fresh_keys, fresh_values, q_gain, freq, group_of, prefix_len, tail_len,
      prompt_key_cache, prompt_value_cache, tail_key_cache, tail_value_cache)
    tiles = half // 128
    sizes = [128 * ((tiles + 2 - i) // 3) for i in range(3)]
    parts = [(sum(sizes[:i]), sizes[i]) for i in range(3)]
    np_ = n * n - 1
    dma = pltpu.SemaphoreType.DMA
    scratch = [
        pltpu.VMEM((np_, heads, per, hd), BF16),
        pltpu.VMEM((np_, per, 128), F32),
        pltpu.VMEM((heads, per, hd), BF16),
        pltpu.VMEM((per, 128), F32),
        pltpu.VMEM((steps, d), BF16),
        pltpu.VMEM(w_out.shape, BF16),
        pltpu.VMEM((256, d), BF16),
        pltpu.VMEM((128, d), BF16),
        pltpu.VMEM((2, steps, d), BF16),
        pltpu.VMEM((2, n, n, n, 8, half), BF16),
        pltpu.VMEM((2, n, n, n, 8, half), BF16),
        pltpu.VMEM((n, n, n, 8, half), BF16),
        pltpu.VMEM((n, n, n, 8, half), BF16),
    ]
    scratch += [pltpu.VMEM((n - 1, n, n, 8, size), BF16) for size in sizes]
    scratch += [pltpu.VMEM((n, n, 8, size), BF16) for size in sizes]
    scratch += [pltpu.VMEM((np_, 8, size), BF16) for size in sizes]
    scratch += [
        pltpu.VMEM((2, 8, half), F32),
        pltpu.VMEM((steps, d), BF16),
        dma((7,)), dma((2, np_)), dma((2, np_)), dma((2,)), dma((2,)), dma((3, np_)), dma((3, np_)),
        dma((3, n - 1)), dma((3, n - 1)), dma((3, n)), dma((3, n)), dma((n,)), dma((n,)),
        dma((3, n - 1)), dma((3, n - 1)), dma((3, np_)), dma((3, np_)),
    ]
    out = pl.pallas_call(
        functools.partial(exchange, n, parts),
        out_shape=jax.ShapeDtypeStruct((1, steps, d), F32),
        in_specs=[ANY] * 2 + [ANY] * 5 + [VMEM] * 3,
        out_specs=VMEM,
        scratch_shapes=scratch,
        compiler_params=pltpu.CompilerParams(collective_id=0, has_side_effects=True),
        name="exchange",
    )(num, st, resid, w_out, w_gate.T, w_up.T, w_down, attn_gain, pre_gain, post_gain)
    return out.astype(BF16)


def solution(mesh):
    in_specs = (
        P("req", None, None), P("req", None, None), P("req", None, None), P(),
        P("req", "seq", None), P("req", "seq", None), P("req", "seq", None), P("req", "seq", None),
        P("req"), P("req"), P("req"), P("req", None, None), P(), P(), P(), P(),
        P(None, ("seq", "req")), P(None, ("seq", "req")), P(("seq", "req"), None),
    )
    n = mesh.shape["req"] // 2
    return jax.shard_map(
        functools.partial(shards, n), mesh=mesh, in_specs=in_specs,
        out_specs=P(("req", "seq"), None, None), check_vma=False,
    )
```

```python
import functools
import jax
import jax.numpy as jnp
from jax import lax
from jax.experimental import pallas as pl
from jax.experimental.pallas import tpu as pltpu
from jax.sharding import PartitionSpec as P

MESH = pl.DeviceIdType.MESH
ANY = pl.BlockSpec(memory_space=pl.ANY)
SMEM = pl.BlockSpec(memory_space=pltpu.SMEM)
VMEM = pl.BlockSpec(memory_space=pltpu.VMEM)
F32 = jnp.float32
BF16 = jnp.bfloat16
eps = 1e-06
theta = 1000000.0
LOW = -3e38
SAFE = -1.5e38


def scale_for_norm(rows, gain):
    mean_square = jnp.mean(rows * rows, axis=-1, keepdims=True)
    return rows * lax.rsqrt(mean_square + eps) * gain


def nt(a, b):
    return lax.dot_general(a, b, (((1,), (1,)), ((), ())), preferred_element_type=F32)


def nn(a, b):
    return jnp.dot(a, b, preferred_element_type=F32)


def cache_copies(pk, pv, tk, tv, kb, vb, tkb, tvb, sems):
    heads, _, _, hd = kb.shape
    copies = []
    for k in range(heads):
        cols = pl.ds(k * hd, hd)
        copies.append([
            pltpu.make_async_copy(pk.at[:, :, cols], kb.at[k], sems.at[k, 0]),
            pltpu.make_async_copy(tk.at[:, :, cols], tkb.at[k], sems.at[k, 1]),
            pltpu.make_async_copy(pv.at[:, :, cols], vb.at[k], sems.at[k, 2]),
            pltpu.make_async_copy(tv.at[:, :, cols], tvb.at[k], sems.at[k, 3]),
        ])
    return copies


def attention(q_ref, fk_ref, fv_ref, gain_ref, freq_ref, group_ref, prefix_ref, tail_ref, num_ref, st_ref,
              kb, vb, tkb, tvb, copies, done):
    requests, steps, _ = q_ref.shape
    heads, groups, block, hd = kb.shape
    tail_block = tkb.shape[2]
    rows = requests * 2 * steps
    per = 2 * steps
    chunk = min(4, requests)
    seq = lax.axis_index("seq")
    ends, tails, members = [], [], []
    for r in range(requests):
        group = group_ref[r]
        end = prefix_ref[0]
        for g in range(1, groups):
            end = jnp.where(group == g, prefix_ref[g], end)
        ends.append(jnp.full((per, 128), end, jnp.int32))
        tails.append(jnp.full((per, 128), tail_ref[r], jnp.int32))
        members.append(jnp.full((per, 128), group, jnp.int32))
    ends, tails, members = (jnp.concatenate(v, axis=0) for v in (ends, tails, members))
    step = lax.broadcasted_iota(jnp.int32, (rows, 128), 0) % steps
    angle = (ends + tails + step).astype(F32) * freq_ref[...].reshape(1, 128)
    cosine, sine = jnp.cos(angle), jnp.sin(angle)
    first = members[:, 0:1] == 0
    prompt_end = ends[:, 0:1]
    tail_end = tails[:, 0:1]
    slot = seq * block + lax.broadcasted_iota(jnp.int32, (rows, block), 1)
    prompt_ok = slot < prompt_end
    width = chunk * tail_block
    row = lax.broadcasted_iota(jnp.int32, (rows, width), 0)
    col = lax.broadcasted_iota(jnp.int32, (rows, width), 1)
    tail_ok = ((row // per) % chunk == col // tail_block) & (
        seq * tail_block + col % tail_block < tail_end
    )
    row = lax.broadcasted_iota(jnp.int32, (rows, rows), 0)
    col = lax.broadcasted_iota(jnp.int32, (rows, rows), 1)
    own_ok = (
        (row // per == col // per) & (col % per <= row % steps) & (row // per == seq)
    )
    half = hd // 2

    def rotate(v):
        a, b = v[:, :half], v[:, half:]
        return jnp.concatenate([a * cosine - b * sine, b * cosine + a * sine], axis=1)

    def doubled(a, b):
        return jnp.concatenate([a.astype(F32), b.astype(F32)], axis=1).reshape(rows, hd)

    lane = lax.broadcasted_iota(jnp.int32, (rows, 128), 1)
    stats = jnp.zeros((rows, 128), F32)
    for k in range(heads):
        q = doubled(q_ref[:, :, 2 * k * hd:(2 * k + 1) * hd], q_ref[:, :, (2 * k + 1) * hd:(2 * k + 2) * hd])
        q = (rotate(scale_for_norm(q, gain_ref[...].reshape(1, hd))) * hd ** (-0.5)).astype(BF16)
        fk = fk_ref[:, :, k * hd:(k + 1) * hd]
        own_key = rotate(scale_for_norm(doubled(fk, fk), 1.0)).astype(BF16)
        fv = fv_ref[:, :, k * hd:(k + 1) * hd]
        own_value = doubled(fv, fv).astype(BF16)
        copies[k][0].wait()
        s = jnp.where(first, nt(q, kb[k, 0]), nt(q, kb[k, 1]))
        s = jnp.where(prompt_ok, s, LOW)
        copies[k][1].wait()
        t = jnp.concatenate(
            [
                nt(q[c * chunk * per:(c + 1) * chunk * per], tkb[k, c * chunk:(c + 1) * chunk].reshape(width, hd))
                for c in range(requests // chunk)
            ],
            axis=0,
        )
        t = jnp.where(tail_ok, t, LOW)
        o = jnp.where(own_ok, nt(q, own_key), LOW)
        peak = jnp.maximum(
            jnp.maximum(jnp.max(s, axis=1, keepdims=True), jnp.max(t, axis=1, keepdims=True)),
            jnp.max(o, axis=1, keepdims=True),
        )
        peak = jnp.maximum(peak, SAFE)
        s = jnp.exp(s - peak)
        t = jnp.exp(t - peak)
        o = jnp.exp(o - peak)
        total = (
            jnp.sum(s, axis=1, keepdims=True) + jnp.sum(t, axis=1, keepdims=True) + jnp.sum(o, axis=1, keepdims=True)
        )
        stats = jnp.where(lane == k, peak, jnp.where(lane == heads + k, total, stats))
        t = t.astype(BF16)
        num = nn(o.astype(BF16), own_value)
        copies[k][2].wait()
        num += nn(jnp.where(first, s, 0.0).astype(BF16), vb[k, 0])
        num += nn(jnp.where(first, 0.0, s).astype(BF16), vb[k, 1])
        copies[k][3].wait()
        num += jnp.concatenate(
            [
                nn(t[c * chunk * per:(c + 1) * chunk * per], tvb[k, c * chunk:(c + 1) * chunk].reshape(width, hd))
                for c in range(requests // chunk)
            ],
            axis=0,
        )
        num_ref[:, k] = num.reshape(requests, per, hd).astype(BF16)
        if k == heads - 1:
            st_ref[...] = stats.reshape(requests, per, 128)
        done(k)


def exchange(n, parts, q_ref, fk_ref, fv_ref, gain_ref, freq_ref, group_ref, prefix_ref, tail_ref, pk, pv, tk, tv,
             resid, wo_h, wg_h, wu_h, wd_h, again, pgain, qgain, out_ref,
             num, st, kb, vb, tkb, tvb, cache_sems, an, ast, res, wo, wgu, wd, nb, x, p, rsib, s,
             r2a, r2b, r2c, ta, tb, tc, r1a, r1b, r1c, dn, hst,
             lsem, asend, arecv, sbs, sbr, s1s, s1r, lns, lnr, xs, xr, p3s, p3r, r2s, r2r, r1s, r1r):
    seq, req = lax.axis_index("seq"), lax.axis_index("req")
    me = (seq // n, seq % n, req // 2)
    c = req % 2
    heads = num.shape[1]
    steps = out_ref.shape[1]
    d = out_ref.shape[2]
    half = d // 2
    ff = wd_h.shape[0]
    r2, t, r1 = (r2a, r2b, r2c), (ta, tb, tc), (r1a, r1b, r1c)

    def device(zxy, core):
        return (zxy[0] * n + zxy[1], zxy[2] * 2 + core)

    def moved(offset):
        return tuple((m + o) % n for m, o in zip(me, offset))

    sibling = device(me, 1 - c)
    line_axis = (2, 0, 1)
    plane_axes = ((0, 1), (1, 2), (0, 2))

    def offset_of(part, dl, da, db):
        o = [0, 0, 0]
        o[line_axis[part]] = dl
        o[plane_axes[part][0]] = da
        o[plane_axes[part][1]] = db
        return tuple(o)

    def line_slice(ref, part, value, cols):
        index = [slice(None)] * 3
        index[line_axis[part]] = value
        return ref.at[(*index, slice(None), cols)]

    plane = [(i, j) for i in range(n) for j in range(n) if (i, j) != (0, 0)]
    partners = [
        (i, j, k) for i in range(n) for j in range(n) for k in range(n)
        if 0 < (i > 0) + (j > 0) + (k > 0) < 3
    ]

    barrier = pltpu.get_barrier_semaphore()
    for o in partners:
        pl.semaphore_signal(barrier, inc=1, device_id=device(moved(o), c), device_id_type=MESH)
    pl.semaphore_signal(barrier, inc=1, device_id=sibling, device_id_type=MESH)
    copies = cache_copies(pk, pv, tk, tv, kb, vb, tkb, tvb, cache_sems)
    for some in copies:
        for copy in some:
            copy.start()
    loads = [
        pltpu.make_async_copy(resid.at[seq], res, lsem.at[0]),
        pltpu.make_async_copy(wg_h, wgu.at[pl.ds(0, ff)], lsem.at[1]),
        pltpu.make_async_copy(wu_h, wgu.at[pl.ds(128, ff)], lsem.at[2]),
        pltpu.make_async_copy(wd_h, wd.at[pl.ds(0, ff)], lsem.at[3]),
        pltpu.make_async_copy(wo_h, wo, lsem.at[4]),
    ]
    for copy in loads:
        copy.start()
    wgu[ff:128, :] = jnp.zeros((128 - ff, d), BF16)
    wgu[128 + ff:256, :] = jnp.zeros((128 - ff, d), BF16)
    wd[ff:128, :] = jnp.zeros((128 - ff, d), BF16)

    def remote(src, dst, send, recv, where):
        copy = pltpu.make_async_remote_copy(
            src_ref=src, dst_ref=dst, send_sem=send, recv_sem=recv, device_id=where, device_id_type=MESH
        )
        copy.start()
        return copy

    sent = []
    attn = []

    def send_head(k):
        if k == 0:
            pl.semaphore_wait(barrier, len(partners) + 1)
        for index, (i, j) in enumerate(plane):
            to = moved((i, j, 0))
            dest = to[0] * n + to[1]
            attn.append(remote(num.at[dest, k], an.at[index, k], asend.at[k, index], arecv.at[k, index], device(to, c)))
            if k == heads - 1:
                attn.append(remote(st.at[dest], ast.at[index], asend.at[heads, index], arecv.at[heads, index],
                                   device(to, c)))

    attention(q_ref, fk_ref, fv_ref, gain_ref, freq_ref, group_ref, prefix_ref, tail_ref, num, st,
              kb, vb, tkb, tvb, copies, send_head)
    sent += attn
    for copy in loads:
        copy.wait()
    for copy in attn:
        copy.wait_recv()
    st_all = [st[seq]] + [ast[i] for i in range(len(plane))]
    peak = functools.reduce(jnp.maximum, st_all)
    shrink = [jnp.exp(v[:, :heads] - peak[:, :heads]) for v in st_all]
    total = sum(w * v[:, heads:2 * heads] for w, v in zip(shrink, st_all))
    proj = None
    hd = num.shape[3]
    for k in range(heads):
        mixed = num[seq, k].astype(F32) * shrink[0][:, k:k + 1]
        for i in range(len(plane)):
            mixed += an[i, k].astype(F32) * shrink[i + 1][:, k:k + 1]
        mixed = (mixed / total[:, k:k + 1]).astype(BF16)
        one = nn(mixed, wo[2 * k * hd:(2 * k + 1) * hd, :])
        two = nn(mixed, wo[(2 * k + 1) * hd:(2 * k + 2) * hd, :])
        term = one[:steps] + two[steps:]
        proj = term if proj is None else proj + term
    hstate = (res[...].astype(F32) + scale_for_norm(proj, again[...].reshape(1, d))).astype(BF16)
    hst[...] = hstate
    nb[c] = scale_for_norm(hstate.astype(F32), pgain[...].reshape(1, d)).astype(BF16)
    copy = remote(nb.at[c], nb.at[c], sbs.at[0], sbr.at[0], sibling)
    sent.append(copy)
    copy.wait_recv()
    both = jnp.concatenate([nb[0].astype(F32), nb[1].astype(F32)], axis=0).astype(BF16)
    x[(c, *me)] = jnp.where(c == 0, both[:, :half], both[:, half:])

    mine = x.at[c]
    first = []
    for part, (at, size) in enumerate(parts):
        cols = pl.ds(at, size)
        block = mine.at[(*me, slice(None), cols)]
        row = []
        for index, (i, j) in enumerate(plane):
            where = device(moved(offset_of(part, 0, i, j)), c)
            row.append(remote(block, block, s1s.at[part, index], s1r.at[part, index], where))
        first.append(row)
        sent += row
    lines, siblings = [], []
    for part, (at, size) in enumerate(parts):
        cols = pl.ds(at, size)
        for copy in first[part]:
            copy.wait_recv()
        piece = line_slice(mine, part, me[line_axis[part]], cols)
        row = []
        for dl in range(1, n):
            where = device(moved(offset_of(part, dl, 0, 0)), c)
            row.append(remote(piece, piece, lns.at[part, dl - 1], lnr.at[part, dl - 1], where))
        siblings.append(remote(piece, piece, xs.at[part, 0], xr.at[part, 0], sibling))
        lines.append(row)
        sent += row
    for dl in sorted(range(1, n), key=lambda v: min(v, n - v)):
        for part, (at, size) in enumerate(parts):
            lines[part][dl - 1].wait_recv()
            source = (me[line_axis[part]] - dl + n) % n
            piece = line_slice(mine, part, source, pl.ds(at, size))
            siblings.append(remote(piece, piece, xs.at[part, dl], xr.at[part, dl], sibling))
    sent += siblings
    for copy in siblings:
        copy.wait_recv()

    count = n * n * 8
    third = []
    for z in range(n):
        gu = nt(x[0, z].reshape(count, half), wgu[:, :half]) + nt(x[1, z].reshape(count, half), wgu[:, half:])
        hidden = (jax.nn.gelu(gu[:, :128], approximate=True) * gu[:, 128:]).astype(BF16)
        down = nn(hidden, wd[...])
        p[0, z] = down[:, :half].astype(BF16).reshape(n, n, 8, half)
        p[1, z] = down[:, half:].astype(BF16).reshape(n, n, 8, half)
        third.append(remote(p.at[1 - c, z], rsib.at[z], p3s.at[z], p3r.at[z], sibling))
    sent += third
    for z in range(n):
        third[z].wait_recv()
        s[z] = (p[c, z].astype(F32) + rsib[z].astype(F32)).astype(BF16)
    second = []
    for part, (at, size) in enumerate(parts):
        row = []
        for dl in range(1, n):
            to = moved(offset_of(part, dl, 0, 0))
            piece = line_slice(s, part, to[line_axis[part]], pl.ds(at, size))
            row.append(remote(piece, r2[part].at[dl - 1], r2s.at[part, dl - 1], r2r.at[part, dl - 1], device(to, c)))
        second.append(row)
        sent += row
    last = []
    for part, (at, size) in enumerate(parts):
        for copy in second[part]:
            copy.wait_recv()
        own = line_slice(s, part, me[line_axis[part]], pl.ds(at, size))
        total = own[...].astype(F32)
        for dl in range(1, n):
            total += r2[part][dl - 1].astype(F32)
        t[part][...] = total.astype(BF16)
        row = []
        for index, (i, j) in enumerate(plane):
            to = moved(offset_of(part, 0, i, j))
            a, b = (to[v] for v in plane_axes[part])
            row.append(remote(t[part].at[a, b], r1[part].at[index], r1s.at[part, index], r1r.at[part, index],
                              device(to, c)))
        last.append(row)
        sent += row
    for part, (at, size) in enumerate(parts):
        for copy in last[part]:
            copy.wait_recv()
        a, b = (me[v] for v in plane_axes[part])
        total = t[part][a, b].astype(F32)
        for index in range(len(plane)):
            total += r1[part][index].astype(F32)
        dn[c, :, at:at + size] = total
    copy = remote(dn.at[c], dn.at[c], sbs.at[1], sbr.at[1], sibling)
    sent.append(copy)
    copy.wait_recv()
    down = jnp.concatenate([dn[0], dn[1]], axis=1)
    down = jnp.where(c == 0, down[:steps], down[steps:])
    out_ref[0] = hst[...].astype(F32) + scale_for_norm(down, qgain[...].reshape(1, d))
    for copy in sent:
        copy.wait_send()


def shards(n, q_new, fresh_keys, fresh_values, q_gain, prompt_key_cache, prompt_value_cache, tail_key_cache,
           tail_value_cache, group_of, prefix_len, tail_len, resid, w_out, attn_gain, pre_gain, post_gain,
           w_gate, w_up, w_down):
    requests, steps, query_width = q_new.shape
    hd = q_gain.shape[0]
    heads = fresh_keys.shape[2] // hd
    groups, block, _ = prompt_key_cache.shape
    tail_block = tail_key_cache.shape[1]
    d = resid.shape[2]
    half = d // 2
    ff = w_gate.shape[1]
    per = 2 * steps
    freq = theta ** (-(jnp.arange(hd // 2, dtype=F32) * 2.0 / hd))
    tiles = half // 128
    sizes = [128 * ((tiles + 2 - i) // 3) for i in range(3)]
    parts = [(sum(sizes[:i]), sizes[i]) for i in range(3)]
    np_ = n * n - 1
    dma = pltpu.SemaphoreType.DMA
    scratch = [
        pltpu.VMEM((requests, heads, per, hd), BF16),
        pltpu.VMEM((requests, per, 128), F32),
        pltpu.VMEM((heads, groups, block, hd), BF16),
        pltpu.VMEM((heads, groups, block, hd), BF16),
        pltpu.VMEM((heads, requests, tail_block, hd), BF16),
        pltpu.VMEM((heads, requests, tail_block, hd), BF16),
        dma((heads, 4)),
        pltpu.VMEM((np_, heads, per, hd), BF16),
        pltpu.VMEM((np_, per, 128), F32),
        pltpu.VMEM((steps, d), BF16),
        pltpu.VMEM(w_out.shape, BF16),
        pltpu.VMEM((256, d), BF16),
        pltpu.VMEM((128, d), BF16),
        pltpu.VMEM((2, steps, d), BF16),
        pltpu.VMEM((2, n, n, n, 8, half), BF16),
        pltpu.VMEM((2, n, n, n, 8, half), BF16),
        pltpu.VMEM((n, n, n, 8, half), BF16),
        pltpu.VMEM((n, n, n, 8, half), BF16),
    ]
    scratch += [pltpu.VMEM((n - 1, n, n, 8, size), BF16) for size in sizes]
    scratch += [pltpu.VMEM((n, n, 8, size), BF16) for size in sizes]
    scratch += [pltpu.VMEM((np_, 8, size), BF16) for size in sizes]
    scratch += [
        pltpu.VMEM((2, 8, half), F32),
        pltpu.VMEM((steps, d), BF16),
        dma((5,)), dma((heads + 1, np_)), dma((heads + 1, np_)), dma((2,)), dma((2,)), dma((3, np_)), dma((3, np_)),
        dma((3, n - 1)), dma((3, n - 1)), dma((3, n)), dma((3, n)), dma((n,)), dma((n,)),
        dma((3, n - 1)), dma((3, n - 1)), dma((3, np_)), dma((3, np_)),
    ]
    out = pl.pallas_call(
        functools.partial(exchange, n, parts),
        out_shape=jax.ShapeDtypeStruct((1, steps, d), F32),
        in_specs=[VMEM] * 5 + [SMEM] * 3 + [ANY] * 9 + [VMEM] * 3,
        out_specs=VMEM,
        scratch_shapes=scratch,
        compiler_params=pltpu.CompilerParams(collective_id=0, has_side_effects=True),
        name="exchange",
    )(q_new, fresh_keys, fresh_values, q_gain, freq, group_of, prefix_len, tail_len,
      prompt_key_cache, prompt_value_cache, tail_key_cache, tail_value_cache, resid, w_out, w_gate.T, w_up.T, w_down, attn_gain, pre_gain, post_gain)
    return out.astype(BF16)


def solution(mesh):
    in_specs = (
        P("req", None, None), P("req", None, None), P("req", None, None), P(),
        P("req", "seq", None), P("req", "seq", None), P("req", "seq", None), P("req", "seq", None),
        P("req"), P("req"), P("req"), P("req", None, None), P(), P(), P(), P(),
        P(None, ("seq", "req")), P(None, ("seq", "req")), P(("seq", "req"), None),
    )
    n = mesh.shape["req"] // 2
    return jax.shard_map(
        functools.partial(shards, n), mesh=mesh, in_specs=in_specs,
        out_specs=P(("req", "seq"), None, None), check_vma=False,
    )
```

```python
import functools
import jax
import jax.numpy as jnp
from jax import lax
from jax.experimental import pallas as pl
from jax.experimental.pallas import tpu as pltpu
from jax.sharding import PartitionSpec as P

MESH = pl.DeviceIdType.MESH
ANY = pl.BlockSpec(memory_space=pl.ANY)
SMEM = pl.BlockSpec(memory_space=pltpu.SMEM)
VMEM = pl.BlockSpec(memory_space=pltpu.VMEM)
F32 = jnp.float32
BF16 = jnp.bfloat16
eps = 1e-06
theta = 1000000.0
LOW = -3e38
SAFE = -1.5e38


def scale_for_norm(rows, gain):
    mean_square = jnp.mean(rows * rows, axis=-1, keepdims=True)
    return rows * lax.rsqrt(mean_square + eps) * gain


def nt(a, b):
    return lax.dot_general(a, b, (((1,), (1,)), ((), ())), preferred_element_type=F32)


def nn(a, b):
    return jnp.dot(a, b, preferred_element_type=F32)


def cache_copies(pk, pv, tk, tv, kb, vb, tkb, tvb, sems):
    heads, _, _, hd = kb.shape
    copies = []
    for k in range(heads):
        cols = pl.ds(k * hd, hd)
        copies.append([
            pltpu.make_async_copy(pk.at[:, :, cols], kb.at[k], sems.at[k, 0]),
            pltpu.make_async_copy(tk.at[:, :, cols], tkb.at[k], sems.at[k, 1]),
            pltpu.make_async_copy(pv.at[:, :, cols], vb.at[k], sems.at[k, 2]),
            pltpu.make_async_copy(tv.at[:, :, cols], tvb.at[k], sems.at[k, 3]),
        ])
    return copies


def attention(q_ref, fk_ref, fv_ref, gain_ref, freq_ref, group_ref, prefix_ref, tail_ref, num_ref, st_ref,
              kb, vb, tkb, tvb, copies, done):
    requests, steps, _ = q_ref.shape
    heads, groups, block, hd = kb.shape
    tail_block = tkb.shape[2]
    rows = requests * 2 * steps
    per = 2 * steps
    chunk = min(4, requests)
    seq = lax.axis_index("seq")
    ends, tails, members = [], [], []
    for r in range(requests):
        group = group_ref[r]
        end = prefix_ref[0]
        for g in range(1, groups):
            end = jnp.where(group == g, prefix_ref[g], end)
        ends.append(jnp.full((per, 128), end, jnp.int32))
        tails.append(jnp.full((per, 128), tail_ref[r], jnp.int32))
        members.append(jnp.full((per, 128), group, jnp.int32))
    ends, tails, members = (jnp.concatenate(v, axis=0) for v in (ends, tails, members))
    step = lax.broadcasted_iota(jnp.int32, (rows, 128), 0) % steps
    angle = (ends + tails + step).astype(F32) * freq_ref[...].reshape(1, 128)
    cosine, sine = jnp.cos(angle), jnp.sin(angle)
    first = members[:, 0:1] == 0
    prompt_end = ends[:, 0:1]
    tail_end = tails[:, 0:1]
    slot = seq * block + lax.broadcasted_iota(jnp.int32, (rows, block), 1)
    prompt_ok = slot < prompt_end
    width = chunk * tail_block
    row = lax.broadcasted_iota(jnp.int32, (rows, width), 0)
    col = lax.broadcasted_iota(jnp.int32, (rows, width), 1)
    tail_ok = ((row // per) % chunk == col // tail_block) & (
        seq * tail_block + col % tail_block < tail_end
    )
    row = lax.broadcasted_iota(jnp.int32, (rows, rows), 0)
    col = lax.broadcasted_iota(jnp.int32, (rows, rows), 1)
    own_ok = (
        (row // per == col // per) & (col % per <= row % steps) & (row // per == seq)
    )
    half = hd // 2

    def rotate(v):
        a, b = v[:, :half], v[:, half:]
        return jnp.concatenate([a * cosine - b * sine, b * cosine + a * sine], axis=1)

    def doubled(a, b):
        return jnp.concatenate([a.astype(F32), b.astype(F32)], axis=1).reshape(rows, hd)

    lane = lax.broadcasted_iota(jnp.int32, (rows, 128), 1)
    stats = jnp.zeros((rows, 128), F32)
    for k in range(heads):
        q = doubled(q_ref[:, :, 2 * k * hd:(2 * k + 1) * hd], q_ref[:, :, (2 * k + 1) * hd:(2 * k + 2) * hd])
        q = (rotate(scale_for_norm(q, gain_ref[...].reshape(1, hd))) * hd ** (-0.5)).astype(BF16)
        fk = fk_ref[:, :, k * hd:(k + 1) * hd]
        own_key = rotate(scale_for_norm(doubled(fk, fk), 1.0)).astype(BF16)
        fv = fv_ref[:, :, k * hd:(k + 1) * hd]
        own_value = doubled(fv, fv).astype(BF16)
        copies[k][0].wait()
        s = jnp.where(first, nt(q, kb[k, 0]), nt(q, kb[k, 1]))
        s = jnp.where(prompt_ok, s, LOW)
        copies[k][1].wait()
        t = jnp.concatenate(
            [
                nt(q[c * chunk * per:(c + 1) * chunk * per], tkb[k, c * chunk:(c + 1) * chunk].reshape(width, hd))
                for c in range(requests // chunk)
            ],
            axis=0,
        )
        t = jnp.where(tail_ok, t, LOW)
        o = jnp.where(own_ok, nt(q, own_key), LOW)
        peak = jnp.maximum(
            jnp.maximum(jnp.max(s, axis=1, keepdims=True), jnp.max(t, axis=1, keepdims=True)),
            jnp.max(o, axis=1, keepdims=True),
        )
        peak = jnp.maximum(peak, SAFE)
        s = jnp.exp(s - peak)
        t = jnp.exp(t - peak)
        o = jnp.exp(o - peak)
        total = (
            jnp.sum(s, axis=1, keepdims=True) + jnp.sum(t, axis=1, keepdims=True) + jnp.sum(o, axis=1, keepdims=True)
        )
        stats = jnp.where(lane == k, peak, jnp.where(lane == heads + k, total, stats))
        t = t.astype(BF16)
        num = nn(o.astype(BF16), own_value)
        copies[k][2].wait()
        num += nn(jnp.where(first, s, 0.0).astype(BF16), vb[k, 0])
        num += nn(jnp.where(first, 0.0, s).astype(BF16), vb[k, 1])
        copies[k][3].wait()
        num += jnp.concatenate(
            [
                nn(t[c * chunk * per:(c + 1) * chunk * per], tvb[k, c * chunk:(c + 1) * chunk].reshape(width, hd))
                for c in range(requests // chunk)
            ],
            axis=0,
        )
        num_ref[:, k] = num.reshape(requests, per, hd).astype(BF16)
        if k == heads - 1:
            st_ref[...] = stats.reshape(requests, per, 128)
        done(k)


def exchange(n, parts, q_ref, fk_ref, fv_ref, gain_ref, freq_ref, group_ref, prefix_ref, tail_ref, pk, pv, tk, tv,
             resid, wo_h, wg_h, wu_h, wd_h, again, pgain, qgain, out_ref,
             num, st, kb, vb, tkb, tvb, cache_sems, an, ast, res, wo, wgu, wd, nb, x, p, rsib, s,
             r2a, r2b, r2c, ta, tb, tc, r1a, r1b, r1c, dn, hst,
             lsem, asend, arecv, sbs, sbr, s1s, s1r, lns, lnr, xs, xr, p3s, p3r, r2s, r2r, r1s, r1r):
    seq, req = lax.axis_index("seq"), lax.axis_index("req")
    me = (seq // n, seq % n, req // 2)
    c = req % 2
    heads = num.shape[1]
    steps = out_ref.shape[1]
    d = out_ref.shape[2]
    half = d // 2
    ff = wd_h.shape[0]
    r2, t, r1 = (r2a, r2b, r2c), (ta, tb, tc), (r1a, r1b, r1c)

    def device(zxy, core):
        return (zxy[0] * n + zxy[1], zxy[2] * 2 + core)

    def moved(offset):
        return tuple((m + o) % n for m, o in zip(me, offset))

    sibling = device(me, 1 - c)
    line_axis = (2, 0, 1)
    plane_axes = ((0, 1), (1, 2), (0, 2))

    def offset_of(part, dl, da, db):
        o = [0, 0, 0]
        o[line_axis[part]] = dl
        o[plane_axes[part][0]] = da
        o[plane_axes[part][1]] = db
        return tuple(o)

    plane = [(i, j) for i in range(n) for j in range(n) if (i, j) != (0, 0)]
    partners = [
        (i, j, k) for i in range(n) for j in range(n) for k in range(n)
        if 0 < (i > 0) + (j > 0) + (k > 0) < 3
    ]

    barrier = pltpu.get_barrier_semaphore()
    for o in partners:
        pl.semaphore_signal(barrier, inc=1, device_id=device(moved(o), c), device_id_type=MESH)
    pl.semaphore_signal(barrier, inc=1, device_id=sibling, device_id_type=MESH)
    copies = cache_copies(pk, pv, tk, tv, kb, vb, tkb, tvb, cache_sems)
    for some in copies:
        for copy in some:
            copy.start()
    loads = [
        pltpu.make_async_copy(resid.at[seq], res, lsem.at[0]),
        pltpu.make_async_copy(wg_h, wgu.at[pl.ds(0, ff)], lsem.at[1]),
        pltpu.make_async_copy(wu_h, wgu.at[pl.ds(128, ff)], lsem.at[2]),
        pltpu.make_async_copy(wd_h, wd.at[pl.ds(0, ff)], lsem.at[3]),
        pltpu.make_async_copy(wo_h, wo, lsem.at[4]),
    ]
    for copy in loads:
        copy.start()
    wgu[ff:128, :] = jnp.zeros((128 - ff, d), BF16)
    wgu[128 + ff:256, :] = jnp.zeros((128 - ff, d), BF16)
    wd[ff:128, :] = jnp.zeros((128 - ff, d), BF16)

    def remote(src, dst, send, recv, where):
        copy = pltpu.make_async_remote_copy(
            src_ref=src, dst_ref=dst, send_sem=send, recv_sem=recv, device_id=where, device_id_type=MESH
        )
        copy.start()
        return copy

    sent = []
    attn = []

    def send_head(k):
        if k == 0:
            pl.semaphore_wait(barrier, len(partners) + 1)
        for index, (i, j) in enumerate(plane):
            to = moved((i, j, 0))
            dest = to[0] * n + to[1]
            attn.append(remote(num.at[dest, k], an.at[index, k], asend.at[k, index], arecv.at[k, index], device(to, c)))
            if k == heads - 1:
                attn.append(remote(st.at[dest], ast.at[index], asend.at[heads, index], arecv.at[heads, index],
                                   device(to, c)))

    attention(q_ref, fk_ref, fv_ref, gain_ref, freq_ref, group_ref, prefix_ref, tail_ref, num, st,
              kb, vb, tkb, tvb, copies, send_head)
    sent += attn
    for copy in loads:
        copy.wait()
    for copy in attn:
        copy.wait_recv()
    st_all = [st[seq]] + [ast[i] for i in range(len(plane))]
    peak = functools.reduce(jnp.maximum, st_all)
    shrink = [jnp.exp(v[:, :heads] - peak[:, :heads]) for v in st_all]
    total = sum(w * v[:, heads:2 * heads] for w, v in zip(shrink, st_all))
    proj = None
    hd = num.shape[3]
    for k in range(heads):
        mixed = num[seq, k].astype(F32) * shrink[0][:, k:k + 1]
        for i in range(len(plane)):
            mixed += an[i, k].astype(F32) * shrink[i + 1][:, k:k + 1]
        mixed = (mixed / total[:, k:k + 1]).astype(BF16)
        one = nn(mixed, wo[2 * k * hd:(2 * k + 1) * hd, :])
        two = nn(mixed, wo[(2 * k + 1) * hd:(2 * k + 2) * hd, :])
        term = one[:steps] + two[steps:]
        proj = term if proj is None else proj + term
    hstate = (res[...].astype(F32) + scale_for_norm(proj, again[...].reshape(1, d))).astype(BF16)
    hst[...] = hstate
    nb[c] = scale_for_norm(hstate.astype(F32), pgain[...].reshape(1, d)).astype(BF16)
    copy = remote(nb.at[c], nb.at[c], sbs.at[0], sbr.at[0], sibling)
    sent.append(copy)
    copy.wait_recv()
    both = jnp.concatenate([nb[0].astype(F32), nb[1].astype(F32)], axis=0).astype(BF16)
    x[(c, *me)] = jnp.where(c == 0, both[:, :half], both[:, half:])

    mine = x.at[c]
    near = sorted(range(n), key=lambda v: (min(v, n - v), v))
    first, lines, passed = {}, {}, {}

    def piece(part, value, group):
        index = [slice(None)] * 3
        index[line_axis[part]] = value
        index[plane_axes[part][0]] = group
        at, size = parts[part]
        return mine.at[(*index, slice(None), pl.ds(at, size))]

    def pass_on(part, dl, g):
        value = (me[line_axis[part]] - dl + n) % n
        group = (me[plane_axes[part][0]] - g + n) % n
        block = piece(part, value, group)
        passed[part, dl, g] = remote(block, block, xs.at[part, g, dl], xr.at[part, g, dl], sibling)

    for i in near:
        for part, (at, size) in enumerate(parts):
            block = mine.at[(*me, slice(None), pl.ds(at, size))]
            for j in near:
                if (i, j) != (0, 0):
                    where = device(moved(offset_of(part, 0, i, j)), c)
                    slot = i * n + j - 1
                    first[part, i, j] = remote(block, block, s1s.at[part, slot], s1r.at[part, slot], where)
    for i in near:
        for part in range(3):
            for j in near:
                if (i, j) != (0, 0):
                    first[part, i, j].wait_recv()
            block = piece(part, me[line_axis[part]], (me[plane_axes[part][0]] - i + n) % n)
            for dl in near[1:]:
                where = device(moved(offset_of(part, dl, 0, 0)), c)
                lines[part, dl, i] = remote(block, block, lns.at[part, i, dl - 1], lnr.at[part, i, dl - 1], where)
            pass_on(part, 0, i)
    sent += list(first.values()) + list(lines.values())

    def forward(dz):
        for v in near:
            for part, dl, g in ((0, v, dz), (1, dz, v), (2, v, dz)):
                if dl:
                    lines[part, dl, g].wait_recv()
                    pass_on(part, dl, g)

    count = n * n * 8
    third, second, last = {}, {}, {}

    def compute(dz):
        z = (me[0] - dz + n) % n
        for v in near:
            for key in ((0, v, dz), (1, dz, v), (2, v, dz)):
                passed[key].wait_recv()
        gu = nt(x[0, z].reshape(count, half), wgu[:, :half]) + nt(x[1, z].reshape(count, half), wgu[:, half:])
        hidden = (jax.nn.gelu(gu[:, :128], approximate=True) * gu[:, 128:]).astype(BF16)
        down = nn(hidden, wd[...])
        p[0, z] = down[:, :half].astype(BF16).reshape(n, n, 8, half)
        p[1, z] = down[:, half:].astype(BF16).reshape(n, n, 8, half)
        third[dz] = remote(p.at[1 - c, z], rsib.at[z], p3s.at[dz], p3r.at[dz], sibling)

    def reduce(dz):
        z = (me[0] - dz + n) % n
        third[dz].wait_recv()
        s[z] = (p[c, z].astype(F32) + rsib[z].astype(F32)).astype(BF16)
        for dl in near[:0:-1]:
            for part in (0, 2):
                at, size = parts[part]
                to = moved(offset_of(part, dl, 0, 0))
                index = [z, slice(None), slice(None)]
                index[line_axis[part]] = to[line_axis[part]]
                second[part, dl, dz] = remote(
                    s.at[(*index, slice(None), pl.ds(at, size))], r2[part].at[dl - 1, z],
                    r2s.at[part, dz, dl - 1], r2r.at[part, dz, dl - 1], device(to, c))
        if dz:
            at, size = parts[1]
            second[1, dz, 0] = remote(
                s.at[z, :, :, :, pl.ds(at, size)], r2[1].at[dz - 1],
                r2s.at[1, 0, dz - 1], r2r.at[1, 0, dz - 1], device((z, me[1], me[2]), c))

    def spread(part, i):
        group = (me[plane_axes[part][0]] + i) % n
        for j in near[::-1]:
            if (i, j) != (0, 0):
                to = moved(offset_of(part, 0, i, j))
                b = to[plane_axes[part][1]]
                slot = i * n + j - 1
                last[part, i, j] = remote(t[part].at[group, b], r1[part].at[slot], r1s.at[part, slot],
                                          r1r.at[part, slot], device(to, c))

    def gather(dz):
        z = (me[0] - dz + n) % n
        for part in (0, 2):
            at, size = parts[part]
            for dl in near[1:]:
                second[part, dl, dz].wait_recv()
            index = [z, slice(None), slice(None)]
            index[line_axis[part]] = me[line_axis[part]]
            total = s[(*index, slice(None), slice(at, at + size))].astype(F32)
            for dl in range(1, n):
                total += r2[part][dl - 1, z].astype(F32)
            t[part][z] = total.astype(BF16)
            spread(part, (n - dz) % n)

    order = near
    forward(order[0])
    forward(order[1])
    compute(order[0])
    forward(order[2])
    compute(order[1])
    reduce(order[0])
    forward(order[3])
    compute(order[2])
    reduce(order[1])
    compute(order[3])
    reduce(order[2])
    gather(order[0])
    reduce(order[3])
    gather(order[1])
    gather(order[2])
    at, size = parts[1]
    for dl in near[1:]:
        second[1, dl, 0].wait_recv()
    total = s[me[0], :, :, :, at:at + size].astype(F32)
    for dl in range(1, n):
        total += r2[1][dl - 1].astype(F32)
    t[1][...] = total.astype(BF16)
    for i in near[::-1]:
        spread(1, i)
    gather(order[3])
    sent += list(passed.values()) + list(third.values()) + list(second.values()) + list(last.values())
    for part, (at, size) in enumerate(parts):
        for key, copy in last.items():
            if key[0] == part:
                copy.wait_recv()
        a, b = (me[v] for v in plane_axes[part])
        total = t[part][a, b].astype(F32)
        for index in range(len(plane)):
            total += r1[part][index].astype(F32)
        dn[c, :, at:at + size] = total
    copy = remote(dn.at[c], dn.at[c], sbs.at[1], sbr.at[1], sibling)
    sent.append(copy)
    copy.wait_recv()
    down = jnp.concatenate([dn[0], dn[1]], axis=1)
    down = jnp.where(c == 0, down[:steps], down[steps:])
    out_ref[0] = hst[...].astype(F32) + scale_for_norm(down, qgain[...].reshape(1, d))
    for copy in sent:
        copy.wait_send()


def shards(n, q_new, fresh_keys, fresh_values, q_gain, prompt_key_cache, prompt_value_cache, tail_key_cache,
           tail_value_cache, group_of, prefix_len, tail_len, resid, w_out, attn_gain, pre_gain, post_gain,
           w_gate, w_up, w_down):
    requests, steps, query_width = q_new.shape
    hd = q_gain.shape[0]
    heads = fresh_keys.shape[2] // hd
    groups, block, _ = prompt_key_cache.shape
    tail_block = tail_key_cache.shape[1]
    d = resid.shape[2]
    half = d // 2
    ff = w_gate.shape[1]
    per = 2 * steps
    freq = theta ** (-(jnp.arange(hd // 2, dtype=F32) * 2.0 / hd))
    tiles = half // 128
    sizes = [128 * ((tiles + 2 - i) // 3) for i in range(3)]
    parts = [(sum(sizes[:i]), sizes[i]) for i in range(3)]
    np_ = n * n - 1
    dma = pltpu.SemaphoreType.DMA
    scratch = [
        pltpu.VMEM((requests, heads, per, hd), BF16),
        pltpu.VMEM((requests, per, 128), F32),
        pltpu.VMEM((heads, groups, block, hd), BF16),
        pltpu.VMEM((heads, groups, block, hd), BF16),
        pltpu.VMEM((heads, requests, tail_block, hd), BF16),
        pltpu.VMEM((heads, requests, tail_block, hd), BF16),
        dma((heads, 4)),
        pltpu.VMEM((np_, heads, per, hd), BF16),
        pltpu.VMEM((np_, per, 128), F32),
        pltpu.VMEM((steps, d), BF16),
        pltpu.VMEM(w_out.shape, BF16),
        pltpu.VMEM((256, d), BF16),
        pltpu.VMEM((128, d), BF16),
        pltpu.VMEM((2, steps, d), BF16),
        pltpu.VMEM((2, n, n, n, 8, half), BF16),
        pltpu.VMEM((2, n, n, n, 8, half), BF16),
        pltpu.VMEM((n, n, n, 8, half), BF16),
        pltpu.VMEM((n, n, n, 8, half), BF16),
    ]
    scratch += [pltpu.VMEM((n - 1, n, n, 8, size), BF16) for size in sizes]
    scratch += [pltpu.VMEM((n, n, 8, size), BF16) for size in sizes]
    scratch += [pltpu.VMEM((np_, 8, size), BF16) for size in sizes]
    scratch += [
        pltpu.VMEM((2, 8, half), F32),
        pltpu.VMEM((steps, d), BF16),
        dma((5,)), dma((heads + 1, np_)), dma((heads + 1, np_)), dma((2,)), dma((2,)), dma((3, np_)), dma((3, np_)),
        dma((3, n, n - 1)), dma((3, n, n - 1)), dma((3, n, n)), dma((3, n, n)), dma((n,)), dma((n,)),
        dma((3, n, n - 1)), dma((3, n, n - 1)), dma((3, np_)), dma((3, np_)),
    ]
    out = pl.pallas_call(
        functools.partial(exchange, n, parts),
        out_shape=jax.ShapeDtypeStruct((1, steps, d), F32),
        in_specs=[VMEM] * 5 + [SMEM] * 3 + [ANY] * 9 + [VMEM] * 3,
        out_specs=VMEM,
        scratch_shapes=scratch,
        compiler_params=pltpu.CompilerParams(collective_id=0, has_side_effects=True),
        name="exchange",
    )(q_new, fresh_keys, fresh_values, q_gain, freq, group_of, prefix_len, tail_len,
      prompt_key_cache, prompt_value_cache, tail_key_cache, tail_value_cache, resid, w_out, w_gate.T, w_up.T, w_down, attn_gain, pre_gain, post_gain)
    return out.astype(BF16)


def solution(mesh):
    in_specs = (
        P("req", None, None), P("req", None, None), P("req", None, None), P(),
        P("req", "seq", None), P("req", "seq", None), P("req", "seq", None), P("req", "seq", None),
        P("req"), P("req"), P("req"), P("req", None, None), P(), P(), P(), P(),
        P(None, ("seq", "req")), P(None, ("seq", "req")), P(("seq", "req"), None),
    )
    n = mesh.shape["req"] // 2
    return jax.shard_map(
        functools.partial(shards, n), mesh=mesh, in_specs=in_specs,
        out_specs=P(("req", "seq"), None, None), check_vma=False,
    )
```
